32 devices in a mesh: gx: 8 (over z, y), gy: 4 (over x, core).
Axes of the slice: x: 2, y: 2, z: 4, core: 2. Of those that a mesh axis runs over, the one named last changes fastest.
Arguments:
- psi: float32 [2, 256, 16, 1024], P(None, 'gx', None, 'gy'), may hold values from -6 to 6
- potential: float32 [256, 16, 1024], P('gx', None, 'gy'), may hold values from 0 to 4
Outputs:
- psi_half: float32 [2, 256, 16, 1024], P(None, 'gx', None, 'gy')
The draws below stay inside these ranges and needn't reach their ends.
All inputs are finite; a program needn't handle non-finite values.
Results may differ from the reference program's by a relative error of at most 0.00005.
Values sent between devices are 32-bit elements; how exact they have to be, the bound alone decides.
A program may use at most 64 MiB of HBM per device.

```python
import jax
import jax.numpy as jnp
from jax import lax

CX = 32
NZ = 16
RYZ = 2
NX = 256
NY = 1024


def draw_psi(key, part):
    values = jax.random.normal(key, (2, NX, NZ, NY), jnp.float32)
    return jnp.clip(values, -6.0, 6.0).astype(jnp.float32)


def level_of(rng, shape, shards, low, largest):
    def one(position, blocks):
        heights = jax.random.uniform(jax.random.fold_in(jax.random.fold_in(rng, 6), position), (blocks,), jnp.float32, low / len(shards), largest / len(shards))
        return jnp.repeat(jnp.exp(heights), shape[position] // blocks).reshape((-1,) + (1,) * (len(shape) - position - 1))

    loudness = one(*shards[0])
    for cut in shards[1:]:
        loudness = loudness * one(*cut)
    return loudness


def setup_inputs(seed: int = 0) -> dict:
    streams_of = jax.random.split(jax.random.key(seed), 3)
    psi = draw_psi(jax.random.fold_in(streams_of[2], 71), 0)
    potential = jnp.clip(4.0 * jax.random.uniform(streams_of[1], (NX, NZ, NY), jnp.float32) ** level_of(streams_of[1], (NX, NZ, NY), ((0, 8), (2, 4)), -0.2, 0.2), 0.0, 4.0)
    return dict(psi=psi, potential=potential)


def neighbours(field, axis):
    width = [(0, 0)] * field.ndim
    width[axis] = (1, 1)
    padded = jnp.pad(field, width)
    upper = lax.slice_in_dim(padded, 2, field.shape[axis] + 2, axis=axis)
    lower = lax.slice_in_dim(padded, 0, field.shape[axis], axis=axis)
    return upper + lower - 2.0 * field


def reference(psi, potential):
    coef = 256.0 * CX * CX
    real_part, imag_part = psi[0], psi[1]
    theta = 0.5 * (potential + real_part * real_part + imag_part * imag_part)
    cosine, sine = jnp.cos(theta), jnp.sin(theta)
    turn_re = real_part * cosine + imag_part * sine
    turn_im = imag_part * cosine - real_part * sine
    side_re = RYZ * (neighbours(turn_re, 2) + neighbours(turn_re, 1))
    side_im = RYZ * (neighbours(turn_im, 2) + neighbours(turn_im, 1))
    rhs_re = 2.0 * turn_re - side_im
    rhs_im = 2.0 * turn_im + side_re

    def forward(carry, row):
        cp_re, cp_im, dp_re, dp_im = carry
        f_re, f_im = row
        m_re = 1.0 - coef * cp_im
        m_im = 2.0 * coef + coef * cp_re
        denom = m_re * m_re + m_im * m_im
        new_cp_re = (-coef * m_im) / denom
        new_cp_im = (-coef * m_re) / denom
        n_re = f_re - coef * dp_im
        n_im = f_im + coef * dp_re
        new_dp_re = (n_re * m_re + n_im * m_im) / denom
        new_dp_im = (n_im * m_re - n_re * m_im) / denom
        out = (new_cp_re, new_cp_im, new_dp_re, new_dp_im)
        return out, out

    start = (jnp.zeros((), jnp.float32), jnp.zeros((), jnp.float32),
             jnp.zeros_like(rhs_re[0]), jnp.zeros_like(rhs_re[0]))
    unused, sweep = lax.scan(forward, start, (rhs_re, rhs_im))

    def backward(carry, row):
        x_re, x_im = carry
        cp_re, cp_im, dp_re, dp_im = row
        new_re = dp_re - (cp_re * x_re - cp_im * x_im)
        new_im = dp_im - (cp_re * x_im + cp_im * x_re)
        return (new_re, new_im), (new_re, new_im)

    unused, solved = lax.scan(backward, (jnp.zeros_like(rhs_re[0]), jnp.zeros_like(rhs_re[0])), sweep, reverse=True)
    return jnp.stack([solved[0] - turn_re, solved[1] - turn_im])
```

```python
import functools

import jax
import jax.numpy as jnp
import numpy as np
from jax import lax
from jax.experimental import pallas as pl
from jax.experimental.pallas import tpu as pltpu
from jax.sharding import PartitionSpec as P

RYZ = 2.0
LANES = 128
MESH = pl.DeviceIdType.MESH


def tables(cells, count):
    coef = 256.0 * cells * cells
    total = cells * count
    lam = np.arccosh(np.complex128(1.0 - 0.5j / coef))
    sh = lambda m: np.sinh(lam * m)
    scale = -(1j / coef) / (sh(1) * sh(total + 1))
    x0 = cells * np.arange(count, dtype=np.float64)
    end = x0 + cells
    f_q = sh(end) - sh(end + 1)
    f_e = sh(end + 1)
    r_q = sh(total + 1 - end) - sh(total - end)
    r_e = sh(total - end)
    w_l = scale * sh(total + 1 - x0)
    w_r = scale * sh(x0)
    d_l = scale * (sh(total - x0) - sh(total + 1 - x0))
    d_r = scale * (sh(x0 + 1) - sh(x0))
    rows = [f_q, f_e, r_q, r_e, w_l, w_r, d_l, d_r]
    place = np.stack([part for row in rows for part in (row.real, row.imag)], axis=1)
    m = np.arange(1, cells + 1, dtype=np.float64)
    g1 = sh(cells + 1 - m) / sh(1)
    ge = g1 - sh(cells - m) / sh(1)
    weights = np.zeros((8, LANES))
    for row, value in enumerate([g1.real, g1.imag, ge.real, ge.imag]):
        weights[row, :cells] = value
    return place.astype(np.float32).reshape(-1), weights.astype(np.float32), coef


def sincos(theta):
    n = jnp.floor(theta * np.float32(2.0 / np.pi) + 0.5)
    r = theta - n * np.float32(1.5703125)
    r = r - n * np.float32(4.837512969970703125e-4)
    r = r - n * np.float32(7.549789954891882e-8)
    r2 = r * r
    s = r2 * np.float32(-1.9515295891e-4) + np.float32(8.3321608736e-3)
    s = s * r2 + np.float32(-1.6666654611e-1)
    s = s * (r2 * r) + r
    c = r2 * np.float32(2.443315711809948e-5) + np.float32(-1.388731625493765e-3)
    c = c * r2 + np.float32(4.166664568298827e-2)
    c = c * (r2 * r2) + (1.0 - 0.5 * r2)
    q = n.astype(jnp.int32)
    odd = (q & 1) == 1
    sine = jnp.where(odd, c, s)
    cosine = jnp.where(odd, s, c)
    sine = jnp.where((q & 2) == 2, -sine, sine)
    cosine = jnp.where(((q + 1) & 2) == 2, -cosine, cosine)
    return sine, cosine


def turn(re, im, pot):
    theta = 0.5 * (pot + re * re + im * im)
    sine, cosine = sincos(theta)
    return re * cosine + im * sine, im * cosine - re * sine


def kernel(count, wide, coef, chunk, psi, pot, place_ref, weights, out, psi_v, pot_v, turned, rho,
           out_v, edge, halo, fr, recv, in_sem, out_sem, hs_sem, hr_sem, s_sem, r_sem):
    cells, planes, lines = pot_v.shape
    chunks = cells // chunk
    gx = lax.axis_index("gx")
    gy = lax.axis_index("gy")
    inv = np.float32(1.0 / coef)

    def load(i):
        part = pl.ds(i * chunk, chunk)
        return (
            pltpu.make_async_copy(psi.at[:, part], psi_v.at[:, part], in_sem.at[0, i]),
            pltpu.make_async_copy(pot.at[part], pot_v.at[part], in_sem.at[1, i]),
        )

    for i in range(chunks):
        for copy in load(i):
            copy.start()

    barrier = pltpu.get_barrier_semaphore()

    @pl.loop(1, count)
    def _(off):
        pl.semaphore_signal(barrier, inc=1, device_id={"gx": lax.rem(gx + off, count)},
                            device_id_type=MESH)

    @pl.when(gy > 0)
    def _():
        pl.semaphore_signal(barrier, inc=1, device_id={"gy": gy - 1}, device_id_type=MESH)

    @pl.when(gy < wide - 1)
    def _():
        pl.semaphore_signal(barrier, inc=1, device_id={"gy": gy + 1}, device_id_type=MESH)

    lane = lax.broadcasted_iota(jnp.int32, (planes, LANES), 1)
    for i in range(chunks):
        for copy in load(i):
            copy.wait()

    def pack(c, acc):
        new = []
        for which in range(3):
            src = (psi_v.at[0, c], psi_v.at[1, c], pot_v.at[c])[which]
            first = src[:, 0:LANES][:, 0:1]
            last = src[:, lines - LANES : lines][:, LANES - 1 : LANES]
            new.append(jnp.where(lane == c, first, acc[2 * which]))
            new.append(jnp.where(lane == c, last, acc[2 * which + 1]))
        return tuple(new)

    zero_edge = jnp.zeros((planes, LANES), jnp.float32)
    packed = lax.fori_loop(0, cells, pack, (zero_edge,) * 6, unroll=4)
    for which in range(3):
        edge[0, which] = packed[2 * which]
        edge[1, which] = packed[2 * which + 1]

    greeted = jnp.where(gy > 0, 1, 0) + jnp.where(gy < wide - 1, 1, 0)
    pl.semaphore_wait(barrier, count - 1 + greeted)

    down = pltpu.make_async_remote_copy(edge.at[0], halo.at[1], hs_sem.at[0], hr_sem.at[1],
                                        device_id={"gy": gy - 1}, device_id_type=MESH)
    up = pltpu.make_async_remote_copy(edge.at[1], halo.at[0], hs_sem.at[1], hr_sem.at[0],
                                      device_id={"gy": gy + 1}, device_id_type=MESH)

    @pl.when(gy > 0)
    def _():
        down.start()

    @pl.when(gy == 0)
    def _():
        halo[0] = jnp.zeros(halo.shape[1:], jnp.float32)

    @pl.when(gy < wide - 1)
    def _():
        up.start()

    @pl.when(gy == wide - 1)
    def _():
        halo[1] = jnp.zeros(halo.shape[1:], jnp.float32)

    def advance(c, carry):
        e_re, e_im, q_re, q_im = carry
        t_re, t_im = turn(psi_v[0, c], psi_v[1, c], pot_v[c])
        turned[0, c] = t_re
        turned[1, c] = t_im
        e_re = e_re + (t_re + inv * q_im)
        e_im = e_im + (t_im - inv * q_re)
        return e_re, e_im, q_re + e_re, q_im + e_im

    zero = jnp.zeros((planes, lines), jnp.float32)
    e_re, e_im, q_re, q_im = lax.fori_loop(0, cells, advance, (zero,) * 4, unroll=2)

    @pl.when(gy > 0)
    def _():
        up.wait_recv()

    @pl.when(gy < wide - 1)
    def _():
        down.wait_recv()

    sides = []
    sums = []
    for side in range(2):
        h_re, h_im = turn(halo[side, 0], halo[side, 1], halo[side, 2])
        sides.append((h_re, h_im))
        g_re, g_im = weights[0:1, :], weights[1:2, :]
        k_re, k_im = weights[2:3, :], weights[3:4, :]
        total = lambda x: jnp.sum(x, axis=1, keepdims=True)
        sums.append((
            (total(k_re * h_re - k_im * h_im), total(k_re * h_im + k_im * h_re)),
            (total(g_re * h_re - g_im * h_im), total(g_re * h_im + g_im * h_re)),
        ))

    col = lax.broadcasted_iota(jnp.int32, (planes, lines), 1)
    row = lax.broadcasted_iota(jnp.int32, (planes, lines), 0)
    at_first, at_last = col == 0, col == lines - 1
    at_bottom, at_top = row == 0, row == planes - 1

    def lap(x, first, last):
        left = jnp.where(at_first, first, pltpu.roll(x, 1, 1))
        right = jnp.where(at_last, last, pltpu.roll(x, lines - 1, 1))
        below = jnp.where(at_bottom, 0.0, pltpu.roll(x, 1, 0))
        above = jnp.where(at_top, 0.0, pltpu.roll(x, planes - 1, 0))
        return ((left + right) + (below + above)) - 4.0 * x

    def stencil(re, im, first, last):
        lap_re = lap(re, first[0], last[0])
        lap_im = lap(im, first[1], last[1])
        return 2.0 * re - RYZ * lap_im, 2.0 * im + RYZ * lap_re

    e_re, e_im = stencil(e_re, e_im, sums[0][0], sums[1][0])
    q_re, q_im = stencil(q_re, q_im, sums[0][1], sums[1][1])

    def scalar(index):
        return place_ref[gx * 16 + 2 * index], place_ref[gx * 16 + 2 * index + 1]

    def both(a, x, b, y):
        return (
            (a[0] * x[0] - a[1] * x[1]) + (b[0] * y[0] - b[1] * y[1]),
            (a[0] * x[1] + a[1] * x[0]) + (b[0] * y[1] + b[1] * y[0]),
        )

    for which in range(2):
        value = both(scalar(2 * which), (q_re, q_im), scalar(2 * which + 1), (e_re, e_im))
        fr[which, 0] = value[0]
        fr[which, 1] = value[1]

    def message(peer):
        return pltpu.make_async_remote_copy(
            fr.at[jnp.where(peer < gx, 1, 0)], recv.at[gx], s_sem.at[peer], r_sem.at[gx],
            device_id={"gx": peer}, device_id_type=MESH)

    @pl.loop(1, count)
    def _(off):
        message(lax.rem(gx + off, count)).start()

    h_all = (sides[0][0], sides[0][1], sides[1][0], sides[1][1])

    def fill(c, h):
        first = (h[0][:, 0:1], h[1][:, 0:1])
        last = (h[2][:, 0:1], h[3][:, 0:1])
        r_re, r_im = stencil(turned[0, c], turned[1, c], first, last)
        rho[0, c] = -inv * r_im
        rho[1, c] = inv * r_re
        return tuple(pltpu.roll(x, LANES - 1, 1) for x in h)

    lax.fori_loop(0, cells, fill, h_all, unroll=2)

    def arrival(k):
        return pltpu.make_async_remote_copy(
            fr.at[0], recv.at[k], s_sem.at[k], r_sem.at[k],
            device_id={"gx": k}, device_id_type=MESH)

    def take(k, acc):
        arrival(k).wait_recv()
        return acc[0] + recv[k, 0], acc[1] + recv[k, 1]

    left = lax.fori_loop(0, gx, take, (zero, zero))
    right = lax.fori_loop(gx + 1, count, take, (fr[1, 0], fr[1, 1]))
    w = both(scalar(4), left, scalar(5), right)
    d = both(scalar(6), left, scalar(7), right)

    def store(i):
        part = pl.ds(i * chunk, chunk)
        return pltpu.make_async_copy(out_v.at[:, part], out.at[:, part], out_sem.at[i])

    def march(c, carry):
        w_re, w_im, d_re, d_im = carry
        w_re = w_re + d_re
        w_im = w_im + d_im
        out_v[0, c] = w_re - turned[0, c]
        out_v[1, c] = w_im - turned[1, c]
        d_re = d_re + (rho[0, c] + inv * w_im)
        d_im = d_im + (rho[1, c] - inv * w_re)
        return w_re, w_im, d_re, d_im

    carry = (w[0], w[1], d[0], d[1])
    for i in range(chunks):
        carry = lax.fori_loop(i * chunk, (i + 1) * chunk, march, carry, unroll=4)
        store(i).start()

    @pl.when(gy > 0)
    def _():
        down.wait_send()

    @pl.when(gy < wide - 1)
    def _():
        up.wait_send()

    @pl.loop(1, count)
    def _(off):
        message(lax.rem(gx + off, count)).wait_send()

    for i in range(chunks):
        store(i).wait()


def shards(psi, potential):
    unused, cells, planes, lines = psi.shape
    count = lax.axis_size("gx")
    wide = lax.axis_size("gy")
    place, weights, coef = tables(cells, count)
    chunk = 8 if cells % 8 == 0 else cells
    chunks = cells // chunk
    block = (2, cells, planes, lines)
    return pl.pallas_call(
        functools.partial(kernel, count, wide, coef, chunk),
        out_shape=jax.ShapeDtypeStruct(block, jnp.float32),
        in_specs=[
            pl.BlockSpec(memory_space=pl.ANY),
            pl.BlockSpec(memory_space=pl.ANY),
            pl.BlockSpec(memory_space=pltpu.SMEM),
            pl.BlockSpec(memory_space=pltpu.VMEM),
        ],
        out_specs=pl.BlockSpec(memory_space=pl.ANY),
        scratch_shapes=[
            pltpu.VMEM(block, jnp.float32),
            pltpu.VMEM(block[1:], jnp.float32),
            pltpu.VMEM(block, jnp.float32),
            pltpu.VMEM(block, jnp.float32),
            pltpu.VMEM(block, jnp.float32),
            pltpu.VMEM((2, 3, planes, LANES), jnp.float32),
            pltpu.VMEM((2, 3, planes, LANES), jnp.float32),
            pltpu.VMEM((2, 2, planes, lines), jnp.float32),
            pltpu.VMEM((count, 2, planes, lines), jnp.float32),
            pltpu.SemaphoreType.DMA((2, chunks)),
            pltpu.SemaphoreType.DMA((chunks,)),
            pltpu.SemaphoreType.DMA((2,)),
            pltpu.SemaphoreType.DMA((2,)),
            pltpu.SemaphoreType.DMA((count,)),
            pltpu.SemaphoreType.DMA((count,)),
        ],
        compiler_params=pltpu.CompilerParams(collective_id=0, has_side_effects=True),
    )(psi, potential, jnp.asarray(place), jnp.asarray(weights))


def solution(mesh):
    return jax.shard_map(
        shards,
        mesh=mesh,
        in_specs=(P(None, "gx", None, "gy"), P("gx", None, "gy")),
        out_specs=P(None, "gx", None, "gy"),
        check_vma=False,
    )
```

```python
import functools

import jax
import jax.numpy as jnp
import numpy as np
from jax import lax
from jax.experimental import pallas as pl
from jax.experimental.pallas import tpu as pltpu
from jax.sharding import PartitionSpec as P

RYZ = 2.0
LANES = 128
MESH = pl.DeviceIdType.MESH


def tables(cells, count):
    coef = 256.0 * cells * cells
    total = cells * count
    lam = np.arccosh(np.complex128(1.0 - 0.5j / coef))
    sh = lambda m: np.sinh(lam * m)
    scale = -(1j / coef) / (sh(1) * sh(total + 1))
    x0 = cells * np.arange(count, dtype=np.float64)
    end = x0 + cells
    f_q = sh(end) - sh(end + 1)
    f_e = sh(end + 1)
    r_q = sh(total + 1 - end) - sh(total - end)
    r_e = sh(total - end)
    w_l = scale * sh(total + 1 - x0)
    w_r = scale * sh(x0)
    d_l = scale * (sh(total - x0) - sh(total + 1 - x0))
    d_r = scale * (sh(x0 + 1) - sh(x0))
    rows = [f_q, f_e, r_q, r_e, w_l, w_r, d_l, d_r]
    place = np.stack([part for row in rows for part in (row.real, row.imag)], axis=1)
    m = np.arange(1, cells + 1, dtype=np.float64)
    g1 = sh(cells + 1 - m) / sh(1)
    ge = g1 - sh(cells - m) / sh(1)
    weights = np.zeros((8, LANES))
    for row, value in enumerate([g1.real, g1.imag, ge.real, ge.imag]):
        weights[row, :cells] = value
    return place.astype(np.float32).reshape(-1), weights.astype(np.float32), coef


def sincos(theta):
    n = jnp.floor(theta * np.float32(2.0 / np.pi) + 0.5)
    r = theta - n * np.float32(1.5703125)
    r = r - n * np.float32(4.837512969970703125e-4)
    r = r - n * np.float32(7.549789954891882e-8)
    r2 = r * r
    s = r2 * np.float32(-1.9515295891e-4) + np.float32(8.3321608736e-3)
    s = s * r2 + np.float32(-1.6666654611e-1)
    s = s * (r2 * r) + r
    c = r2 * np.float32(2.443315711809948e-5) + np.float32(-1.388731625493765e-3)
    c = c * r2 + np.float32(4.166664568298827e-2)
    c = c * (r2 * r2) + (1.0 - 0.5 * r2)
    q = n.astype(jnp.int32)
    odd = (q & 1) == 1
    sine = jnp.where(odd, c, s)
    cosine = jnp.where(odd, s, c)
    sine = jnp.where((q & 2) == 2, -sine, sine)
    cosine = jnp.where(((q + 1) & 2) == 2, -cosine, cosine)
    return sine, cosine


def turn(re, im, pot):
    theta = 0.5 * (pot + re * re + im * im)
    sine, cosine = sincos(theta)
    return re * cosine + im * sine, im * cosine - re * sine


def kernel(count, wide, coef, chunk, psi, pot, place_in, weights_in, turned, rho,
           start, place_ref, weights, table_sem, psi_v, pot_v, edge, halo, fr, recv, in_sem, hs_sem, hr_sem, s_sem, r_sem):
    cells, planes, lines = pot_v.shape
    chunks = cells // chunk
    gx = lax.axis_index("gx")
    gy = lax.axis_index("gy")
    inv = np.float32(1.0 / coef)

    def load(i):
        part = pl.ds(i * chunk, chunk)
        return (
            pltpu.make_async_copy(psi.at[:, part], psi_v.at[:, part], in_sem.at[0, i]),
            pltpu.make_async_copy(pot.at[part], pot_v.at[part], in_sem.at[1, i]),
        )

    for i in range(chunks):
        for copy in load(i):
            copy.start()

    constants = (
        pltpu.make_async_copy(place_in, place_ref, table_sem.at[0]),
        pltpu.make_async_copy(weights_in, weights, table_sem.at[1]),
    )
    for copy in constants:
        copy.start()

    barrier = pltpu.get_barrier_semaphore()

    @pl.loop(1, count)
    def _(off):
        pl.semaphore_signal(barrier, inc=1, device_id={"gx": lax.rem(gx + off, count)},
                            device_id_type=MESH)

    @pl.when(gy > 0)
    def _():
        pl.semaphore_signal(barrier, inc=1, device_id={"gy": gy - 1}, device_id_type=MESH)

    @pl.when(gy < wide - 1)
    def _():
        pl.semaphore_signal(barrier, inc=1, device_id={"gy": gy + 1}, device_id_type=MESH)

    lane = lax.broadcasted_iota(jnp.int32, (planes, LANES), 1)
    for i in range(chunks):
        for copy in load(i):
            copy.wait()

    def pack(c, acc):
        new = []
        for which in range(3):
            src = (psi_v.at[0, c], psi_v.at[1, c], pot_v.at[c])[which]
            first = src[:, 0:LANES][:, 0:1]
            last = src[:, lines - LANES : lines][:, LANES - 1 : LANES]
            new.append(jnp.where(lane == c, first, acc[2 * which]))
            new.append(jnp.where(lane == c, last, acc[2 * which + 1]))
        return tuple(new)

    zero_edge = jnp.zeros((planes, LANES), jnp.float32)
    packed = lax.fori_loop(0, cells, pack, (zero_edge,) * 6, unroll=4)
    for which in range(3):
        edge[0, which] = packed[2 * which]
        edge[1, which] = packed[2 * which + 1]

    def advance(c, carry):
        e_re, e_im, q_re, q_im = carry
        t_re, t_im = turn(psi_v[0, c], psi_v[1, c], pot_v[c])
        turned[0, c] = t_re
        turned[1, c] = t_im
        e_re = e_re + (t_re + inv * q_im)
        e_im = e_im + (t_im - inv * q_re)
        return e_re, e_im, q_re + e_re, q_im + e_im

    zero = jnp.zeros((planes, lines), jnp.float32)
    e_re, e_im, q_re, q_im = lax.fori_loop(0, cells, advance, (zero,) * 4, unroll=2)

    for copy in constants:
        copy.wait()
    greeted = jnp.where(gy > 0, 1, 0) + jnp.where(gy < wide - 1, 1, 0)
    pl.semaphore_wait(barrier, count - 1 + greeted)

    down = pltpu.make_async_remote_copy(edge.at[0], halo.at[1], hs_sem.at[0], hr_sem.at[1],
                                        device_id={"gy": gy - 1}, device_id_type=MESH)
    up = pltpu.make_async_remote_copy(edge.at[1], halo.at[0], hs_sem.at[1], hr_sem.at[0],
                                      device_id={"gy": gy + 1}, device_id_type=MESH)

    @pl.when(gy > 0)
    def _():
        down.start()

    @pl.when(gy == 0)
    def _():
        halo[0] = jnp.zeros(halo.shape[1:], jnp.float32)

    @pl.when(gy < wide - 1)
    def _():
        up.start()

    @pl.when(gy == wide - 1)
    def _():
        halo[1] = jnp.zeros(halo.shape[1:], jnp.float32)

    @pl.when(gy > 0)
    def _():
        up.wait_recv()

    @pl.when(gy < wide - 1)
    def _():
        down.wait_recv()

    sides = []
    sums = []
    for side in range(2):
        h_re, h_im = turn(halo[side, 0], halo[side, 1], halo[side, 2])
        sides.append((h_re, h_im))
        g_re, g_im = weights[0:1, :], weights[1:2, :]
        k_re, k_im = weights[2:3, :], weights[3:4, :]
        total = lambda x: jnp.sum(x, axis=1, keepdims=True)
        sums.append((
            (total(k_re * h_re - k_im * h_im), total(k_re * h_im + k_im * h_re)),
            (total(g_re * h_re - g_im * h_im), total(g_re * h_im + g_im * h_re)),
        ))

    col = lax.broadcasted_iota(jnp.int32, (planes, lines), 1)
    row = lax.broadcasted_iota(jnp.int32, (planes, lines), 0)
    at_first, at_last = col == 0, col == lines - 1
    at_bottom, at_top = row == 0, row == planes - 1

    def lap(x, first, last):
        left = jnp.where(at_first, first, pltpu.roll(x, 1, 1))
        right = jnp.where(at_last, last, pltpu.roll(x, lines - 1, 1))
        below = jnp.where(at_bottom, 0.0, pltpu.roll(x, 1, 0))
        above = jnp.where(at_top, 0.0, pltpu.roll(x, planes - 1, 0))
        return ((left + right) + (below + above)) - 4.0 * x

    def stencil(re, im, first, last):
        lap_re = lap(re, first[0], last[0])
        lap_im = lap(im, first[1], last[1])
        return 2.0 * re - RYZ * lap_im, 2.0 * im + RYZ * lap_re

    e_re, e_im = stencil(e_re, e_im, sums[0][0], sums[1][0])
    q_re, q_im = stencil(q_re, q_im, sums[0][1], sums[1][1])

    def scalar(index):
        return place_ref[gx * 16 + 2 * index], place_ref[gx * 16 + 2 * index + 1]

    def both(a, x, b, y):
        return (
            (a[0] * x[0] - a[1] * x[1]) + (b[0] * y[0] - b[1] * y[1]),
            (a[0] * x[1] + a[1] * x[0]) + (b[0] * y[1] + b[1] * y[0]),
        )

    for which in range(2):
        value = both(scalar(2 * which), (q_re, q_im), scalar(2 * which + 1), (e_re, e_im))
        fr[which, 0] = value[0]
        fr[which, 1] = value[1]

    def message(peer):
        return pltpu.make_async_remote_copy(
            fr.at[jnp.where(peer < gx, 1, 0)], recv.at[gx], s_sem.at[peer], r_sem.at[gx],
            device_id={"gx": peer}, device_id_type=MESH)

    @pl.loop(1, count)
    def _(off):
        message(lax.rem(gx + off, count)).start()

    h_all = (sides[0][0], sides[0][1], sides[1][0], sides[1][1])

    def fill(c, h):
        first = (h[0][:, 0:1], h[1][:, 0:1])
        last = (h[2][:, 0:1], h[3][:, 0:1])
        r_re, r_im = stencil(turned[0, c], turned[1, c], first, last)
        rho[0, c] = -inv * r_im
        rho[1, c] = inv * r_re
        return tuple(pltpu.roll(x, LANES - 1, 1) for x in h)

    lax.fori_loop(0, cells, fill, h_all, unroll=2)

    def arrival(k):
        return pltpu.make_async_remote_copy(
            fr.at[0], recv.at[k], s_sem.at[k], r_sem.at[k],
            device_id={"gx": k}, device_id_type=MESH)

    def take(k, acc):
        arrival(k).wait_recv()
        return acc[0] + recv[k, 0], acc[1] + recv[k, 1]

    left = lax.fori_loop(0, gx, take, (zero, zero))
    right = lax.fori_loop(gx + 1, count, take, (fr[1, 0], fr[1, 1]))
    w = both(scalar(4), left, scalar(5), right)
    d = both(scalar(6), left, scalar(7), right)

    for index, value in enumerate(w + d):
        start[index] = value

    @pl.when(gy > 0)
    def _():
        down.wait_send()

    @pl.when(gy < wide - 1)
    def _():
        up.wait_send()

    @pl.loop(1, count)
    def _(off):
        message(lax.rem(gx + off, count)).wait_send()


def finish(coef, chunk, turned, rho, start, out, out_v, out_sem):
    cells = turned.shape[1]
    chunks = cells // chunk
    inv = np.float32(1.0 / coef)

    def store(i):
        part = pl.ds(i * chunk, chunk)
        return pltpu.make_async_copy(out_v.at[:, part], out.at[:, part], out_sem.at[i])

    def march(c, carry):
        w_re, w_im, d_re, d_im = carry
        w_re = w_re + d_re
        w_im = w_im + d_im
        out_v[0, c] = w_re - turned[0, c]
        out_v[1, c] = w_im - turned[1, c]
        d_re = d_re + (rho[0, c] + inv * w_im)
        d_im = d_im + (rho[1, c] - inv * w_re)
        return w_re, w_im, d_re, d_im

    carry = (start[0], start[1], start[2], start[3])
    for i in range(chunks):
        carry = lax.fori_loop(i * chunk, (i + 1) * chunk, march, carry, unroll=4)
        store(i).start()
    for i in range(chunks):
        store(i).wait()


def shards(psi, potential):
    unused, cells, planes, lines = psi.shape
    count = lax.axis_size("gx")
    wide = lax.axis_size("gy")
    place, weights, coef = tables(cells, count)
    chunk = 8 if cells % 8 == 0 else cells
    chunks = cells // chunk
    block = (2, cells, planes, lines)
    plane = (planes, lines)
    vmem = pl.BlockSpec(memory_space=pltpu.VMEM)
    held = pl.pallas_call(
        functools.partial(kernel, count, wide, coef, chunk),
        out_shape=[
            jax.ShapeDtypeStruct(block, jnp.float32),
            jax.ShapeDtypeStruct(block, jnp.float32),
            jax.ShapeDtypeStruct((4,) + plane, jnp.float32),
        ],
        in_specs=[
            pl.BlockSpec(memory_space=pltpu.HBM),
            pl.BlockSpec(memory_space=pltpu.HBM),
            pl.BlockSpec(memory_space=pltpu.HBM),
            pl.BlockSpec(memory_space=pltpu.HBM),
        ],
        out_specs=[vmem] * 3,
        scratch_shapes=[
            pltpu.SMEM(place.shape, jnp.float32),
            pltpu.VMEM(weights.shape, jnp.float32),
            pltpu.SemaphoreType.DMA((2,)),
            pltpu.VMEM(block, jnp.float32),
            pltpu.VMEM(block[1:], jnp.float32),
            pltpu.VMEM((2, 3, planes, LANES), jnp.float32),
            pltpu.VMEM((2, 3, planes, LANES), jnp.float32),
            pltpu.VMEM((2, 2) + plane, jnp.float32),
            pltpu.VMEM((count, 2) + plane, jnp.float32),
            pltpu.SemaphoreType.DMA((2, chunks)),
            pltpu.SemaphoreType.DMA((2,)),
            pltpu.SemaphoreType.DMA((2,)),
            pltpu.SemaphoreType.DMA((count,)),
            pltpu.SemaphoreType.DMA((count,)),
        ],
        compiler_params=pltpu.CompilerParams(
            collective_id=0, has_side_effects=True, vmem_limit_bytes=24 * 2**20
        ),
    )(psi, potential, jnp.asarray(place), jnp.asarray(weights))
    return pl.pallas_call(
        functools.partial(finish, coef, chunk),
        out_shape=jax.ShapeDtypeStruct(block, jnp.float32),
        in_specs=[vmem] * 3,
        out_specs=pl.BlockSpec(memory_space=pl.ANY),
        scratch_shapes=[
            pltpu.VMEM(block, jnp.float32),
            pltpu.SemaphoreType.DMA((chunks,)),
        ],
        compiler_params=pltpu.CompilerParams(vmem_limit_bytes=16 * 2**20),
    )(*held)


def solution(mesh):
    return jax.shard_map(
        shards,
        mesh=mesh,
        in_specs=(P(None, "gx", None, "gy"), P("gx", None, "gy")),
        out_specs=P(None, "gx", None, "gy"),
        check_vma=False,
    )
```

```python
import functools

import jax
import jax.numpy as jnp
import numpy as np
from jax import lax
from jax.experimental import pallas as pl
from jax.experimental.pallas import tpu as pltpu
from jax.sharding import PartitionSpec as P

RYZ = 2.0
LANES = 128
MESH = pl.DeviceIdType.MESH


def tables(cells, count):
    coef = 256.0 * cells * cells
    total = cells * count
    lam = np.arccosh(np.complex128(1.0 - 0.5j / coef))
    sh = lambda m: np.sinh(lam * m)
    scale = -(1j / coef) / (sh(1) * sh(total + 1))
    x0 = cells * np.arange(count, dtype=np.float64)
    end = x0 + cells
    f_q = sh(end) - sh(end + 1)
    f_e = sh(end + 1)
    r_q = sh(total + 1 - end) - sh(total - end)
    r_e = sh(total - end)
    w_l = scale * sh(total + 1 - x0)
    w_r = scale * sh(x0)
    d_l = scale * (sh(total - x0) - sh(total + 1 - x0))
    d_r = scale * (sh(x0 + 1) - sh(x0))
    rows = [f_q, f_e, r_q, r_e, w_l, w_r, d_l, d_r]
    place = np.stack([part for row in rows for part in (row.real, row.imag)], axis=1)
    m = np.arange(1, cells + 1, dtype=np.float64)
    g1 = sh(cells + 1 - m) / sh(1)
    ge = g1 - sh(cells - m) / sh(1)
    weights = np.zeros((8, LANES))
    for row, value in enumerate([g1.real, g1.imag, ge.real, ge.imag]):
        weights[row, :cells] = value
    return place.astype(np.float32).reshape(-1), weights.astype(np.float32), coef


def sincos(theta):
    n = jnp.floor(theta * np.float32(2.0 / np.pi) + 0.5)
    r = theta - n * np.float32(1.5703125)
    r = r - n * np.float32(4.837512969970703125e-4)
    r = r - n * np.float32(7.549789954891882e-8)
    r2 = r * r
    s = r2 * np.float32(-1.9515295891e-4) + np.float32(8.3321608736e-3)
    s = s * r2 + np.float32(-1.6666654611e-1)
    s = s * (r2 * r) + r
    c = r2 * np.float32(2.443315711809948e-5) + np.float32(-1.388731625493765e-3)
    c = c * r2 + np.float32(4.166664568298827e-2)
    c = c * (r2 * r2) + (1.0 - 0.5 * r2)
    q = n.astype(jnp.int32)
    odd = (q & 1) == 1
    sine = jnp.where(odd, c, s)
    cosine = jnp.where(odd, s, c)
    sine = jnp.where((q & 2) == 2, -sine, sine)
    cosine = jnp.where(((q + 1) & 2) == 2, -cosine, cosine)
    return sine, cosine


def turn(re, im, pot):
    theta = 0.5 * (pot + re * re + im * im)
    sine, cosine = sincos(theta)
    return re * cosine + im * sine, im * cosine - re * sine


def kernel(count, wide, coef, chunk, psi, pot, place_in, weights_in, turned, rho,
           start, place_ref, weights, table_sem, psi_v, pot_v, edge, halo, fr, recv, in_sem, hs_sem, hr_sem, s_sem, r_sem):
    cells, planes, lines = pot_v.shape
    chunks = cells // chunk
    gx = lax.axis_index("gx")
    gy = lax.axis_index("gy")
    inv = np.float32(1.0 / coef)

    def load(i):
        part = pl.ds(i * chunk, chunk)
        return (
            pltpu.make_async_copy(psi.at[:, part], psi_v.at[:, part], in_sem.at[0, i]),
            pltpu.make_async_copy(pot.at[part], pot_v.at[part], in_sem.at[1, i]),
        )

    for i in range(chunks):
        for copy in load(i):
            copy.start()

    constants = (
        pltpu.make_async_copy(place_in, place_ref, table_sem.at[0]),
        pltpu.make_async_copy(weights_in, weights, table_sem.at[1]),
    )
    for copy in constants:
        copy.start()

    barrier = pltpu.get_barrier_semaphore()

    @pl.loop(1, count)
    def _(off):
        pl.semaphore_signal(barrier, inc=1, device_id={"gx": lax.rem(gx + off, count)},
                            device_id_type=MESH)

    @pl.when(gy > 0)
    def _():
        pl.semaphore_signal(barrier, inc=1, device_id={"gy": gy - 1}, device_id_type=MESH)

    @pl.when(gy < wide - 1)
    def _():
        pl.semaphore_signal(barrier, inc=1, device_id={"gy": gy + 1}, device_id_type=MESH)

    lane = lax.broadcasted_iota(jnp.int32, (planes, LANES), 1)
    for i in range(chunks):
        for copy in load(i):
            copy.wait()

    def pack(c, acc):
        new = []
        for which in range(3):
            src = (psi_v.at[0, c], psi_v.at[1, c], pot_v.at[c])[which]
            first = src[:, 0:LANES][:, 0:1]
            last = src[:, lines - LANES : lines][:, LANES - 1 : LANES]
            new.append(jnp.where(lane == c, first, acc[2 * which]))
            new.append(jnp.where(lane == c, last, acc[2 * which + 1]))
        return tuple(new)

    zero_edge = jnp.zeros((planes, LANES), jnp.float32)
    packed = lax.fori_loop(0, cells, pack, (zero_edge,) * 6, unroll=4)
    for which in range(3):
        edge[0, which] = packed[2 * which]
        edge[1, which] = packed[2 * which + 1]

    def advance(c, carry):
        e_re, e_im, q_re, q_im = carry
        t_re, t_im = turn(psi_v[0, c], psi_v[1, c], pot_v[c])
        turned[0, c] = t_re
        turned[1, c] = t_im
        e_re = e_re + (t_re + inv * q_im)
        e_im = e_im + (t_im - inv * q_re)
        return e_re, e_im, q_re + e_re, q_im + e_im

    zero = jnp.zeros((planes, lines), jnp.float32)
    e_re, e_im, q_re, q_im = lax.fori_loop(0, cells, advance, (zero,) * 4, unroll=2)

    for copy in constants:
        copy.wait()
    greeted = jnp.where(gy > 0, 1, 0) + jnp.where(gy < wide - 1, 1, 0)
    pl.semaphore_wait(barrier, count - 1 + greeted)

    down = pltpu.make_async_remote_copy(edge.at[0], halo.at[1], hs_sem.at[0], hr_sem.at[1],
                                        device_id={"gy": gy - 1}, device_id_type=MESH)
    up = pltpu.make_async_remote_copy(edge.at[1], halo.at[0], hs_sem.at[1], hr_sem.at[0],
                                      device_id={"gy": gy + 1}, device_id_type=MESH)

    @pl.when(gy > 0)
    def _():
        down.start()

    @pl.when(gy == 0)
    def _():
        halo[0] = jnp.zeros(halo.shape[1:], jnp.float32)

    @pl.when(gy < wide - 1)
    def _():
        up.start()

    @pl.when(gy == wide - 1)
    def _():
        halo[1] = jnp.zeros(halo.shape[1:], jnp.float32)

    @pl.when(gy > 0)
    def _():
        up.wait_recv()

    @pl.when(gy < wide - 1)
    def _():
        down.wait_recv()

    sides = []
    sums = []
    for side in range(2):
        h_re, h_im = turn(halo[side, 0], halo[side, 1], halo[side, 2])
        sides.append((h_re, h_im))
        g_re, g_im = weights[0:1, :], weights[1:2, :]
        k_re, k_im = weights[2:3, :], weights[3:4, :]
        total = lambda x: jnp.sum(x, axis=1, keepdims=True)
        sums.append((
            (total(k_re * h_re - k_im * h_im), total(k_re * h_im + k_im * h_re)),
            (total(g_re * h_re - g_im * h_im), total(g_re * h_im + g_im * h_re)),
        ))

    col = lax.broadcasted_iota(jnp.int32, (planes, lines), 1)
    row = lax.broadcasted_iota(jnp.int32, (planes, lines), 0)
    at_first, at_last = col == 0, col == lines - 1
    at_bottom, at_top = row == 0, row == planes - 1

    def lap(x, first, last):
        left = jnp.where(at_first, first, pltpu.roll(x, 1, 1))
        right = jnp.where(at_last, last, pltpu.roll(x, lines - 1, 1))
        below = jnp.where(at_bottom, 0.0, pltpu.roll(x, 1, 0))
        above = jnp.where(at_top, 0.0, pltpu.roll(x, planes - 1, 0))
        return ((left + right) + (below + above)) - 4.0 * x

    def stencil(re, im, first, last):
        lap_re = lap(re, first[0], last[0])
        lap_im = lap(im, first[1], last[1])
        return 2.0 * re - RYZ * lap_im, 2.0 * im + RYZ * lap_re

    e_re, e_im = stencil(e_re, e_im, sums[0][0], sums[1][0])
    q_re, q_im = stencil(q_re, q_im, sums[0][1], sums[1][1])

    def scalar(index):
        return place_ref[gx * 16 + 2 * index], place_ref[gx * 16 + 2 * index + 1]

    def both(a, x, b, y):
        return (
            (a[0] * x[0] - a[1] * x[1]) + (b[0] * y[0] - b[1] * y[1]),
            (a[0] * x[1] + a[1] * x[0]) + (b[0] * y[1] + b[1] * y[0]),
        )

    for which in range(2):
        value = both(scalar(2 * which), (q_re, q_im), scalar(2 * which + 1), (e_re, e_im))
        fr[which, 0] = value[0]
        fr[which, 1] = value[1]

    def message(peer):
        return pltpu.make_async_remote_copy(
            fr.at[jnp.where(peer < gx, 1, 0)], recv.at[gx], s_sem.at[peer], r_sem.at[gx],
            device_id={"gx": peer}, device_id_type=MESH)

    @pl.loop(1, count)
    def _(off):
        message(lax.rem(gx + off, count)).start()

    h_all = (sides[0][0], sides[0][1], sides[1][0], sides[1][1])

    def fill(c, h):
        first = (h[0][:, 0:1], h[1][:, 0:1])
        last = (h[2][:, 0:1], h[3][:, 0:1])
        r_re, r_im = stencil(turned[0, c], turned[1, c], first, last)
        rho[0, c] = -inv * r_im
        rho[1, c] = inv * r_re
        return tuple(pltpu.roll(x, LANES - 1, 1) for x in h)

    lax.fori_loop(0, cells, fill, h_all, unroll=2)

    def arrival(k):
        return pltpu.make_async_remote_copy(
            fr.at[0], recv.at[k], s_sem.at[k], r_sem.at[k],
            device_id={"gx": k}, device_id_type=MESH)

    def take(k, acc):
        arrival(k).wait_recv()
        return acc[0] + recv[k, 0], acc[1] + recv[k, 1]

    left = lax.fori_loop(0, gx, take, (zero, zero))
    right = lax.fori_loop(gx + 1, count, take, (fr[1, 0], fr[1, 1]))
    w = both(scalar(4), left, scalar(5), right)
    d = both(scalar(6), left, scalar(7), right)

    for index, value in enumerate(w + d):
        start[index] = value

    @pl.when(gy > 0)
    def _():
        down.wait_send()

    @pl.when(gy < wide - 1)
    def _():
        up.wait_send()

    @pl.loop(1, count)
    def _(off):
        message(lax.rem(gx + off, count)).wait_send()


def finish(coef, chunk, turned, rho, start, out, out_v, out_sem):
    cells = turned.shape[1]
    chunks = cells // chunk
    inv = np.float32(1.0 / coef)

    def store(i):
        part = pl.ds(i * chunk, chunk)
        return pltpu.make_async_copy(out_v.at[:, part], out.at[:, part], out_sem.at[i])

    def march(c, carry):
        w_re, w_im, d_re, d_im = carry
        w_re = w_re + d_re
        w_im = w_im + d_im
        out_v[0, c] = w_re - turned[0, c]
        out_v[1, c] = w_im - turned[1, c]
        d_re = d_re + (rho[0, c] + inv * w_im)
        d_im = d_im + (rho[1, c] - inv * w_re)
        return w_re, w_im, d_re, d_im

    carry = (start[0], start[1], start[2], start[3])
    for i in range(chunks):
        carry = lax.fori_loop(i * chunk, (i + 1) * chunk, march, carry, unroll=4)
        store(i).start()
    for i in range(chunks):
        store(i).wait()


def shards(psi, potential):
    unused, cells, planes, lines = psi.shape
    count = lax.axis_size("gx")
    wide = lax.axis_size("gy")
    place, weights, coef = tables(cells, count)
    chunk = 8 if cells % 8 == 0 else cells
    chunks = cells // chunk
    block = (2, cells, planes, lines)
    plane = (planes, lines)
    vmem = pl.BlockSpec(memory_space=pltpu.VMEM)
    held = pl.pallas_call(
        functools.partial(kernel, count, wide, coef, chunk),
        out_shape=[
            jax.ShapeDtypeStruct(block, jnp.float32),
            jax.ShapeDtypeStruct(block, jnp.float32),
            jax.ShapeDtypeStruct((4,) + plane, jnp.float32),
        ],
        in_specs=[
            pl.BlockSpec(memory_space=pltpu.HBM),
            pl.BlockSpec(memory_space=pltpu.HBM),
            pl.BlockSpec(memory_space=pltpu.HBM),
            pl.BlockSpec(memory_space=pltpu.HBM),
        ],
        out_specs=[vmem] * 3,
        scratch_shapes=[
            pltpu.SMEM(place.shape, jnp.float32),
            pltpu.VMEM(weights.shape, jnp.float32),
            pltpu.SemaphoreType.DMA((2,)),
            pltpu.VMEM(block, jnp.float32),
            pltpu.VMEM(block[1:], jnp.float32),
            pltpu.VMEM((2, 3, planes, LANES), jnp.float32),
            pltpu.VMEM((2, 3, planes, LANES), jnp.float32),
            pltpu.VMEM((2, 2) + plane, jnp.float32),
            pltpu.VMEM((count, 2) + plane, jnp.float32),
            pltpu.SemaphoreType.DMA((2, chunks)),
            pltpu.SemaphoreType.DMA((2,)),
            pltpu.SemaphoreType.DMA((2,)),
            pltpu.SemaphoreType.DMA((count,)),
            pltpu.SemaphoreType.DMA((count,)),
        ],
        compiler_params=pltpu.CompilerParams(
            collective_id=0, has_side_effects=True, vmem_limit_bytes=24 * 2**20
        ),
    )(*(pltpu.with_memory_space_constraint(x, pltpu.HBM) for x in
        (psi, potential, jnp.asarray(place), jnp.asarray(weights))))
    return pl.pallas_call(
        functools.partial(finish, coef, chunk),
        out_shape=jax.ShapeDtypeStruct(block, jnp.float32),
        in_specs=[vmem] * 3,
        out_specs=pl.BlockSpec(memory_space=pl.ANY),
        scratch_shapes=[
            pltpu.VMEM(block, jnp.float32),
            pltpu.SemaphoreType.DMA((chunks,)),
        ],
        compiler_params=pltpu.CompilerParams(vmem_limit_bytes=16 * 2**20),
    )(*held)


def solution(mesh):
    return jax.shard_map(
        shards,
        mesh=mesh,
        in_specs=(P(None, "gx", None, "gy"), P("gx", None, "gy")),
        out_specs=P(None, "gx", None, "gy"),
        check_vma=False,
    )
```

```python
import functools

import jax
import jax.numpy as jnp
import numpy as np
from jax import lax
from jax.experimental import pallas as pl
from jax.experimental.pallas import tpu as pltpu
from jax.sharding import PartitionSpec as P

RYZ = 2.0
LANES = 128
MESH = pl.DeviceIdType.MESH


def tables(cells, count):
    coef = 256.0 * cells * cells
    total = cells * count
    lam = np.arccosh(np.complex128(1.0 - 0.5j / coef))
    sh = lambda m: np.sinh(lam * m)
    scale = -(1j / coef) / (sh(1) * sh(total + 1))
    x0 = cells * np.arange(count, dtype=np.float64)
    end = x0 + cells
    f_q = sh(end) - sh(end + 1)
    f_e = sh(end + 1)
    r_q = sh(total + 1 - end) - sh(total - end)
    r_e = sh(total - end)
    w_l = scale * sh(total + 1 - x0)
    w_r = scale * sh(x0)
    d_l = scale * (sh(total - x0) - sh(total + 1 - x0))
    d_r = scale * (sh(x0 + 1) - sh(x0))
    rows = [f_q, f_e, r_q, r_e, w_l, w_r, d_l, d_r]
    place = np.stack([part for row in rows for part in (row.real, row.imag)], axis=1)
    m = np.arange(1, cells + 1, dtype=np.float64)
    g1 = sh(cells + 1 - m) / sh(1)
    ge = g1 - sh(cells - m) / sh(1)
    weights = np.zeros((8, LANES))
    for row, value in enumerate([g1.real, g1.imag, ge.real, ge.imag]):
        weights[row, :cells] = value
    return place.astype(np.float32).reshape(-1), weights.astype(np.float32), coef


def sincos(theta):
    n = jnp.floor(theta * np.float32(2.0 / np.pi) + 0.5)
    r = theta - n * np.float32(1.5703125)
    r = r - n * np.float32(4.837512969970703125e-4)
    r = r - n * np.float32(7.549789954891882e-8)
    r2 = r * r
    s = r2 * np.float32(-1.9515295891e-4) + np.float32(8.3321608736e-3)
    s = s * r2 + np.float32(-1.6666654611e-1)
    s = s * (r2 * r) + r
    c = r2 * np.float32(2.443315711809948e-5) + np.float32(-1.388731625493765e-3)
    c = c * r2 + np.float32(4.166664568298827e-2)
    c = c * (r2 * r2) + (1.0 - 0.5 * r2)
    q = n.astype(jnp.int32)
    odd = (q & 1) == 1
    sine = jnp.where(odd, c, s)
    cosine = jnp.where(odd, s, c)
    sine = jnp.where((q & 2) == 2, -sine, sine)
    cosine = jnp.where(((q + 1) & 2) == 2, -cosine, cosine)
    return sine, cosine


def turn(re, im, pot):
    theta = 0.5 * (pot + re * re + im * im)
    sine, cosine = sincos(theta)
    return re * cosine + im * sine, im * cosine - re * sine


def kernel(count, wide, coef, chunk, psi, pot, place_in, weights_in, turned, rho,
           start, place_ref, weights, table_sem, psi_v, pot_v, edge, halo, fr, recv, in_sem, hs_sem, hr_sem, s_sem, r_sem,
           fx, fx_recv, fs_sem, fr_sem):
    cells, planes, lines = pot_v.shape
    chunks = cells // chunk
    gx = lax.axis_index("gx")
    gy = lax.axis_index("gy")
    inv = np.float32(1.0 / coef)

    def load(i):
        part = pl.ds(i * chunk, chunk)
        return (
            pltpu.make_async_copy(psi.at[:, part], psi_v.at[:, part], in_sem.at[0, i]),
            pltpu.make_async_copy(pot.at[part], pot_v.at[part], in_sem.at[1, i]),
        )

    for i in range(chunks):
        for copy in load(i):
            copy.start()

    constants = (
        pltpu.make_async_copy(place_in, place_ref, table_sem.at[0]),
        pltpu.make_async_copy(weights_in, weights, table_sem.at[1]),
    )
    for copy in constants:
        copy.start()

    barrier = pltpu.get_barrier_semaphore()

    @pl.loop(1, count)
    def _(off):
        pl.semaphore_signal(barrier, inc=1, device_id={"gx": lax.rem(gx + off, count)},
                            device_id_type=MESH)

    @pl.when(gy > 0)
    def _():
        pl.semaphore_signal(barrier, inc=1, device_id={"gy": gy - 1}, device_id_type=MESH)

    @pl.when(gy < wide - 1)
    def _():
        pl.semaphore_signal(barrier, inc=1, device_id={"gy": gy + 1}, device_id_type=MESH)

    lane = lax.broadcasted_iota(jnp.int32, (planes, LANES), 1)
    for i in range(chunks):
        for copy in load(i):
            copy.wait()

    def pack(c, acc):
        new = []
        for which in range(3):
            src = (psi_v.at[0, c], psi_v.at[1, c], pot_v.at[c])[which]
            first = src[:, 0:LANES][:, 0:1]
            last = src[:, lines - LANES : lines][:, LANES - 1 : LANES]
            new.append(jnp.where(lane == c, first, acc[2 * which]))
            new.append(jnp.where(lane == c, last, acc[2 * which + 1]))
        return tuple(new)

    zero_edge = jnp.zeros((planes, LANES), jnp.float32)
    packed = lax.fori_loop(0, cells, pack, (zero_edge,) * 6, unroll=4)
    for which in range(3):
        edge[0, which] = packed[2 * which]
        edge[1, which] = packed[2 * which + 1]

    def advance(c, carry):
        e_re, e_im, q_re, q_im = carry
        t_re, t_im = turn(psi_v[0, c], psi_v[1, c], pot_v[c])
        turned[0, c] = t_re
        turned[1, c] = t_im
        e_re = e_re + (t_re + inv * q_im)
        e_im = e_im + (t_im - inv * q_re)
        return e_re, e_im, q_re + e_re, q_im + e_im

    zero = jnp.zeros((planes, lines), jnp.float32)
    e_re, e_im, q_re, q_im = lax.fori_loop(0, cells, advance, (zero,) * 4, unroll=2)

    for copy in constants:
        copy.wait()

    col = lax.broadcasted_iota(jnp.int32, (planes, lines), 1)
    row = lax.broadcasted_iota(jnp.int32, (planes, lines), 0)
    at_first, at_last = col == 0, col == lines - 1
    at_bottom, at_top = row == 0, row == planes - 1

    def lap(x, first, last):
        left = jnp.where(at_first, first, pltpu.roll(x, 1, 1))
        right = jnp.where(at_last, last, pltpu.roll(x, lines - 1, 1))
        below = jnp.where(at_bottom, 0.0, pltpu.roll(x, 1, 0))
        above = jnp.where(at_top, 0.0, pltpu.roll(x, planes - 1, 0))
        return ((left + right) + (below + above)) - 4.0 * x

    def stencil(re, im, first, last):
        lap_re = lap(re, first[0], last[0])
        lap_im = lap(im, first[1], last[1])
        return 2.0 * re - RYZ * lap_im, 2.0 * im + RYZ * lap_re

    e_re, e_im = stencil(e_re, e_im, (0.0, 0.0), (0.0, 0.0))
    q_re, q_im = stencil(q_re, q_im, (0.0, 0.0), (0.0, 0.0))

    def scalar(index):
        return place_ref[gx * 16 + 2 * index], place_ref[gx * 16 + 2 * index + 1]

    def both(a, x, b, y):
        return (
            (a[0] * x[0] - a[1] * x[1]) + (b[0] * y[0] - b[1] * y[1]),
            (a[0] * x[1] + a[1] * x[0]) + (b[0] * y[1] + b[1] * y[0]),
        )

    for which in range(2):
        value = both(scalar(2 * which), (q_re, q_im), scalar(2 * which + 1), (e_re, e_im))
        fr[which, 0] = value[0]
        fr[which, 1] = value[1]

    greeted = jnp.where(gy > 0, 1, 0) + jnp.where(gy < wide - 1, 1, 0)
    pl.semaphore_wait(barrier, count - 1 + greeted)

    down = pltpu.make_async_remote_copy(edge.at[0], halo.at[1], hs_sem.at[0], hr_sem.at[1],
                                        device_id={"gy": gy - 1}, device_id_type=MESH)
    up = pltpu.make_async_remote_copy(edge.at[1], halo.at[0], hs_sem.at[1], hr_sem.at[0],
                                      device_id={"gy": gy + 1}, device_id_type=MESH)

    @pl.when(gy > 0)
    def _():
        down.start()

    @pl.when(gy == 0)
    def _():
        halo[0] = jnp.zeros(halo.shape[1:], jnp.float32)

    @pl.when(gy < wide - 1)
    def _():
        up.start()

    @pl.when(gy == wide - 1)
    def _():
        halo[1] = jnp.zeros(halo.shape[1:], jnp.float32)

    def message(peer):
        return pltpu.make_async_remote_copy(
            fr.at[jnp.where(peer < gx, 1, 0)], recv.at[gx], s_sem.at[peer], r_sem.at[gx],
            device_id={"gx": peer}, device_id_type=MESH)

    @pl.loop(1, count)
    def _(off):
        message(lax.rem(gx + off, count)).start()

    @pl.when(gy > 0)
    def _():
        up.wait_recv()

    @pl.when(gy < wide - 1)
    def _():
        down.wait_recv()

    sides = []
    sums = []
    for side in range(2):
        h_re, h_im = turn(halo[side, 0], halo[side, 1], halo[side, 2])
        sides.append((h_re, h_im))
        g_re, g_im = weights[0:1, :], weights[1:2, :]
        k_re, k_im = weights[2:3, :], weights[3:4, :]
        total = lambda x: jnp.sum(x, axis=1, keepdims=True)
        sums.append((
            (total(k_re * h_re - k_im * h_im), total(k_re * h_im + k_im * h_re)),
            (total(g_re * h_re - g_im * h_im), total(g_re * h_im + g_im * h_re)),
        ))

    def turned_sum(value):
        return -2.0 * value[1], 2.0 * value[0]

    for which in range(2):
        tile = zero_edge
        for side in range(2):
            value = both(scalar(2 * which), turned_sum(sums[side][1]),
                         scalar(2 * which + 1), turned_sum(sums[side][0]))
            tile = jnp.where(lane == 2 * side, value[0], tile)
            tile = jnp.where(lane == 2 * side + 1, value[1], tile)
        fx[which] = tile

    def fixing(peer):
        return pltpu.make_async_remote_copy(
            fx.at[jnp.where(peer < gx, 1, 0)], fx_recv.at[gx], fs_sem.at[peer], fr_sem.at[gx],
            device_id={"gx": peer}, device_id_type=MESH)

    @pl.loop(1, count)
    def _(off):
        fixing(lax.rem(gx + off, count)).start()

    h_all = (sides[0][0], sides[0][1], sides[1][0], sides[1][1])

    def fill(c, h):
        first = (h[0][:, 0:1], h[1][:, 0:1])
        last = (h[2][:, 0:1], h[3][:, 0:1])
        r_re, r_im = stencil(turned[0, c], turned[1, c], first, last)
        rho[0, c] = -inv * r_im
        rho[1, c] = inv * r_re
        return tuple(pltpu.roll(x, LANES - 1, 1) for x in h)

    lax.fori_loop(0, cells, fill, h_all, unroll=2)

    def arrival(k):
        return pltpu.make_async_remote_copy(
            fr.at[0], recv.at[k], s_sem.at[k], r_sem.at[k],
            device_id={"gx": k}, device_id_type=MESH)

    def fix_arrival(k):
        return pltpu.make_async_remote_copy(
            fx.at[0], fx_recv.at[k], fs_sem.at[k], fr_sem.at[k],
            device_id={"gx": k}, device_id_type=MESH)

    def take(k, acc):
        arrival(k).wait_recv()
        return acc[0] + recv[k, 0], acc[1] + recv[k, 1]

    def take_fix(k, acc):
        fix_arrival(k).wait_recv()
        return acc + fx_recv[k]

    def spread(value, tile):
        return tuple(
            value[part]
            + jnp.where(at_first, tile[:, part : part + 1], 0.0)
            + jnp.where(at_last, tile[:, 2 + part : 3 + part], 0.0)
            for part in range(2))

    left = lax.fori_loop(0, gx, take, (zero, zero))
    right = lax.fori_loop(gx + 1, count, take, (fr[1, 0], fr[1, 1]))
    left = spread(left, lax.fori_loop(0, gx, take_fix, zero_edge))
    right = spread(right, lax.fori_loop(gx + 1, count, take_fix, fx[1]))
    w = both(scalar(4), left, scalar(5), right)
    d = both(scalar(6), left, scalar(7), right)

    for index, value in enumerate(w + d):
        start[index] = value

    @pl.when(gy > 0)
    def _():
        down.wait_send()

    @pl.when(gy < wide - 1)
    def _():
        up.wait_send()

    @pl.loop(1, count)
    def _(off):
        message(lax.rem(gx + off, count)).wait_send()
        fixing(lax.rem(gx + off, count)).wait_send()


def finish(coef, chunk, turned, rho, start, out, out_v, out_sem):
    cells = turned.shape[1]
    chunks = cells // chunk
    inv = np.float32(1.0 / coef)

    def store(i):
        part = pl.ds(i * chunk, chunk)
        return pltpu.make_async_copy(out_v.at[:, part], out.at[:, part], out_sem.at[i])

    def march(c, carry):
        w_re, w_im, d_re, d_im = carry
        w_re = w_re + d_re
        w_im = w_im + d_im
        out_v[0, c] = w_re - turned[0, c]
        out_v[1, c] = w_im - turned[1, c]
        d_re = d_re + (rho[0, c] + inv * w_im)
        d_im = d_im + (rho[1, c] - inv * w_re)
        return w_re, w_im, d_re, d_im

    carry = (start[0], start[1], start[2], start[3])
    for i in range(chunks):
        carry = lax.fori_loop(i * chunk, (i + 1) * chunk, march, carry, unroll=4)
        store(i).start()
    for i in range(chunks):
        store(i).wait()


def shards(psi, potential):
    unused, cells, planes, lines = psi.shape
    count = lax.axis_size("gx")
    wide = lax.axis_size("gy")
    place, weights, coef = tables(cells, count)
    chunk = 8 if cells % 8 == 0 else cells
    chunks = cells // chunk
    block = (2, cells, planes, lines)
    plane = (planes, lines)
    vmem = pl.BlockSpec(memory_space=pltpu.VMEM)
    held = pl.pallas_call(
        functools.partial(kernel, count, wide, coef, chunk),
        out_shape=[
            jax.ShapeDtypeStruct(block, jnp.float32),
            jax.ShapeDtypeStruct(block, jnp.float32),
            jax.ShapeDtypeStruct((4,) + plane, jnp.float32),
        ],
        in_specs=[
            pl.BlockSpec(memory_space=pltpu.HBM),
            pl.BlockSpec(memory_space=pltpu.HBM),
            pl.BlockSpec(memory_space=pltpu.HBM),
            pl.BlockSpec(memory_space=pltpu.HBM),
        ],
        out_specs=[vmem] * 3,
        scratch_shapes=[
            pltpu.SMEM(place.shape, jnp.float32),
            pltpu.VMEM(weights.shape, jnp.float32),
            pltpu.SemaphoreType.DMA((2,)),
            pltpu.VMEM(block, jnp.float32),
            pltpu.VMEM(block[1:], jnp.float32),
            pltpu.VMEM((2, 3, planes, LANES), jnp.float32),
            pltpu.VMEM((2, 3, planes, LANES), jnp.float32),
            pltpu.VMEM((2, 2) + plane, jnp.float32),
            pltpu.VMEM((count, 2) + plane, jnp.float32),
            pltpu.SemaphoreType.DMA((2, chunks)),
            pltpu.SemaphoreType.DMA((2,)),
            pltpu.SemaphoreType.DMA((2,)),
            pltpu.SemaphoreType.DMA((count,)),
            pltpu.SemaphoreType.DMA((count,)),
            pltpu.VMEM((2, planes, LANES), jnp.float32),
            pltpu.VMEM((count, planes, LANES), jnp.float32),
            pltpu.SemaphoreType.DMA((count,)),
            pltpu.SemaphoreType.DMA((count,)),
        ],
        compiler_params=pltpu.CompilerParams(
            collective_id=0, has_side_effects=True, vmem_limit_bytes=24 * 2**20
        ),
    )(*(pltpu.with_memory_space_constraint(x, pltpu.HBM) for x in
        (psi, potential, jnp.asarray(place), jnp.asarray(weights))))
    return pl.pallas_call(
        functools.partial(finish, coef, chunk),
        out_shape=jax.ShapeDtypeStruct(block, jnp.float32),
        in_specs=[vmem] * 3,
        out_specs=pl.BlockSpec(memory_space=pl.ANY),
        scratch_shapes=[
            pltpu.VMEM(block, jnp.float32),
            pltpu.SemaphoreType.DMA((chunks,)),
        ],
        compiler_params=pltpu.CompilerParams(vmem_limit_bytes=16 * 2**20),
    )(*held)


def solution(mesh):
    return jax.shard_map(
        shards,
        mesh=mesh,
        in_specs=(P(None, "gx", None, "gy"), P("gx", None, "gy")),
        out_specs=P(None, "gx", None, "gy"),
        check_vma=False,
    )
```
